32 devices in a mesh: groups: 2 (over x), row: 16 (over z, y, core).
Axes of the slice: x: 2, y: 2, z: 4, core: 2. Of those that a mesh axis runs over, the one named last changes fastest.
Arguments:
- orbitals: bfloat16 [4096, 512], P(('groups', 'row')), parts along dimension 0, may hold values from -1.296875 to 1.296875
- basis: bfloat16 [4096, 1024], P(('groups', 'row')), parts along dimension 0, may hold values from -0.1875 to 0.1875
- kernel: bfloat16 [4096, 2048], P(('groups', 'row')), parts along dimension 0, may hold values from -6 to 6
Outputs:
- exchange_matrix: float32 [2048, 1024], P('groups', 'row'), parts along dimension 0
The draws below stay inside these ranges and needn't reach their ends.
There are 2 independent parts, one for each index of `groups`. The reference program is written for one: setup_inputs(seed, part) draws one part's arguments, and reference() takes and returns one part's arrays. A program takes and returns all parts, laid end to end along the dimension named above; each array names one. Nothing has to cross between parts.
All inputs are finite; a program needn't handle non-finite values.
Results may differ from the reference program's by a relative error of at most 0.0041.
Values may be sent and summed in bfloat16 or wider, within the bound.
A program may use at most 128 MiB of HBM per device.

```python
import jax
import jax.numpy as jnp
from jax import lax

NOCC = 512
NB = 1024
NP = 2048


def spiked(entries, stream_key, source, target, parts, factor):
    owner, partner = [(jnp.arange(entries.shape[axis_at]) // (entries.shape[axis_at] // parts)).reshape([-1 if axis == axis_at else 1 for axis in range(entries.ndim)]) for axis_at in (source, target)]
    chosen = jax.random.permutation(stream_key, parts)[partner]
    strong = (owner == chosen) | (owner == (partner + parts // 2) % parts)
    return jnp.where(strong, factor * entries, entries)


def steps_of(own_key, shape, split, smallest, high):
    def one(dim, parts):
        draws = jax.random.uniform(jax.random.fold_in(jax.random.fold_in(own_key, 6), dim), (parts,), jnp.float32, smallest / len(split), high / len(split))
        return jnp.repeat(jnp.exp(draws), shape[dim] // parts).reshape((-1,) + (1,) * (len(shape) - dim - 1))

    loudness = one(*split[0])
    for cut in split[1:]:
        loudness = loudness * one(*cut)
    return loudness


def noise(stream_key, shape, spread, most, shards=(), kind=jnp.bfloat16):
    drawn = spread * jax.random.normal(stream_key, shape, jnp.float32)
    if shards:
        drawn = drawn * steps_of(stream_key, shape, shards, -0.22, 0.18)
    return jnp.clip(drawn, -most, most).astype(kind)


def noise_with(stream_key, extent, scale, reach, cuts, heavy, held_as=jnp.bfloat16):
    result = scale * jax.random.normal(stream_key, extent, jnp.float32)
    if cuts:
        result = result * steps_of(stream_key, extent, cuts, -0.22, 0.18)
    return jnp.clip(spiked(result, jax.random.fold_in(stream_key, 3), *heavy), -reach, reach).astype(held_as)


def setup_inputs(seed: int = 0, part: int = 0) -> dict:
    streams_of = jax.random.split(jax.random.key(seed), 4)
    part_splits = jax.random.split(jax.random.fold_in(streams_of[3], part), 4)
    return {
        "orbitals": noise(part_splits[0], (NP, NOCC), 0.21, 1.296875, ((0, 16),)),
        "basis": noise_with(part_splits[1], (NP, NB), NP ** -0.5, 0.1875, ((0, 16),), (0, 1, 16, 2.0)),
        "kernel": noise(part_splits[2], (NP, NP), 1.0, 6.0, ((0, 16),)),
    }


def reference(orbitals, basis, kernel):
    density = lax.dot_general(orbitals, orbitals, (((1,), (1,)), ((), ())), preferred_element_type=jnp.float32)
    weighted = (density * kernel.astype(jnp.float32)).astype(jnp.bfloat16)
    applied = jnp.dot(weighted, basis, preferred_element_type=jnp.float32).astype(jnp.bfloat16)
    return lax.dot_general(basis, applied, (((0,), (0,)), ((), ())), preferred_element_type=jnp.float32)
```

```python
import functools

import jax
import jax.numpy as jnp
from jax import lax
from jax.experimental import pallas as pl
from jax.experimental.pallas import tpu as pltpu
from jax.sharding import PartitionSpec as P

LANES = 128
LEAD, LEAD_Y, LATE, ACROSS = (0, 7, 7), (0, 7, 7), 0, (2.1, 5.6)
MESH = pl.DeviceIdType.MESH
OPARTS, STEP, HOP, AHEAD, LAZY, MOVED, AGE = 2, 14, 32, 60, 60, 1, 4


def layout(mesh):
    n = mesh.shape["row"]
    try:
        line = mesh.devices[0]
        places = [tuple(d.coords) + (d.core_on_chip,) for d in line]
    except AttributeError:
        return n, 1, 1
    cores = len({p[-1] for p in places})
    axes = [a for a in range(3) if len({p[a] for p in places}) > 1]
    sizes = {a: len({p[a] for p in places}) for a in axes}
    for axis_z in axes:
        rest = [a for a in axes if a != axis_z]
        if len(rest) > 1 or (rest and sizes[rest[0]] != 2):
            continue
        y_size = sizes[rest[0]] if rest else 1
        z0 = min(p[axis_z] for p in places)
        y0 = min(p[rest[0]] for p in places) if rest else 0
        found = [
            ((p[axis_z] - z0) * y_size + (p[rest[0]] - y0 if rest else 0)) * cores + p[-1]
            for p in places
        ]
        if found == list(range(n)):
            return sizes[axis_z], y_size, cores
    return n, 1, 1


def kernel(
    dims, o_in, b_in, k_in, out_ref,
    o_all, b_all, k_v, w, app_t, got, in_sem, send_sem, recv_sem, a2a_send, a2a_recv,
):
    Z, Y, C = dims
    n = Z * Y * C
    units = Z * Y
    parts = 3
    rows = o_in.shape[0]
    half_cols = b_all.shape[-1]
    groups = half_cols // LANES
    cw = app_t.shape[0] * app_t.shape[1] // n
    per = LANES // cw

    me = lax.axis_index("row")
    c = me % C
    y = (me // C) % Y
    z = me // (C * Y)
    peer_y = (Y - 1) - y

    def index(zz, yy, cc):
        return (zz * Y + yy) * C + cc

    up_dev = index(jnp.minimum(z + 1, Z - 1), y, c)
    down_dev = index(jnp.maximum(z - 1, 0), y, c)
    y_dev = index(z, peer_y, c)
    sib_dev = index(z, y, (C - 1) - c)
    has_up = z < Z - 1
    has_down = z > 0

    def chunk(i, p):
        return o_all.at[i] if p == 0 else b_all.at[p - 1, i]

    def copy(i, p, kind):
        dev = (up_dev, down_dev, y_dev, sib_dev)[kind]
        return pltpu.make_async_remote_copy(
            src_ref=chunk(i, p),
            dst_ref=chunk(i, p),
            send_sem=send_sem.at[kind, p, i // C],
            recv_sem=recv_sem.at[p, i],
            device_id={"row": dev},
            device_id_type=MESH,
        )

    def wait_recv(i, p):
        copy(i, p, 3).wait_recv()

    loads = [pltpu.make_async_copy(o_in, o_all.at[me], in_sem.at[0])]
    for g in range(2 * groups):
        h, s = g % 2, g // 2
        loads.append(
            pltpu.make_async_copy(
                b_in.at[:, pl.ds(g * LANES, LANES)],
                b_all.at[h, me, :, pl.ds(s * LANES, LANES)],
                in_sem.at[1 + g],
            )
        )
    k_load = pltpu.make_async_copy(k_in, k_v, in_sem.at[1 + 2 * groups])
    for load in loads:
        load.start()
    k_load.start()

    barrier = pltpu.get_barrier_semaphore()

    def greet(dev):
        pl.semaphore_signal(barrier, inc=1, device_id={"row": dev}, device_id_type=MESH)

    pl.when(has_up)(lambda: greet(up_dev))
    pl.when(has_down)(lambda: greet(down_dev))
    if Y > 1:
        greet(y_dev)
    if C > 1:
        greet(sib_dev)
    others = (Y > 1) + (C > 1)
    pl.semaphore_wait(barrier, others + has_up.astype(jnp.int32) + has_down.astype(jnp.int32))

    relays = Y > 1 and Z >= 4
    both, either = jnp.logical_and, jnp.logical_or

    def goes_across(zz, p):
        if not relays:
            return True
        turn = c == p % C
        end = either(both(both(z == 0, zz == 1), turn), both(both(z == Z - 1, zz == Z - 2), turn))
        beside = either(both(z == 1, zz == 0), both(z == Z - 2, zz == Z - 1))
        return jnp.logical_not(either(end, beside))

    def relay_up(p):
        return either(z == 0, both(z == Z - 2, c == p % C))

    def relay_down(p):
        return either(z == Z - 1, both(z == 1, c == p % C))

    def spread(i, zz, p, up=False, down=False, across=False):
        if up:
            pl.when(has_up)(lambda: copy(i, p, 0).start())
        if down:
            pl.when(has_down)(lambda: copy(i, p, 1).start())
        if across and Y > 1:
            pl.when(goes_across(zz, p))(lambda: copy(i, p, 2).start())
        if C > 1:
            copy(i, p, 3).start()

    def own(p):
        if p == 0:
            loads[0].wait()
        else:
            for g in range(2 * groups):
                if g % 2 == p - 1:
                    loads[1 + g].wait()
        pl.when(has_up)(lambda: copy(me, p, 0).start())
        pl.when(has_down)(lambda: copy(me, p, 1).start())
        if C > 1:
            copy(me, p, 3).start()

    def own_across(p):
        copy(me, p, 2).start()

    def along(p, t):
        def low():
            i = index(z - t, y, c)
            wait_recv(i, p)
            spread(i, z - t, p, up=True, across=True)

        def high():
            i = index(z + t, y, c)
            wait_recv(i, p)
            spread(i, z + t, p, down=True, across=True)

        pl.when(z - t >= 0)(low)
        pl.when(z + t < Z)(high)

    def across(p, t):
        def one(zz):
            i = index(zz, peer_y, c)
            wait_recv(i, p)
            if relays and t == 0:
                pl.when(relay_up(p))(lambda: copy(i, p, 0).start())
                pl.when(relay_down(p))(lambda: copy(i, p, 1).start())
            spread(i, zz, p)

        if t == 0:
            one(z)
        else:
            pl.when(z - t >= 0)(lambda: one(z - t))
            pl.when(z + t < Z)(lambda: one(z + t))

    stride = (Z - 0.5) if relays else (Z if Y > 1 else max(Z - 1, 1))
    events = []
    for p in range(parts):
        base = p * stride
        events.append((base - LEAD[p], p, functools.partial(own, p)))
        for t in range(1, Z):
            events.append((base + t + LATE * (t > 1), p, functools.partial(along, p, t)))
        if Y > 1:
            events.append((base - LEAD_Y[p] + 0.01, p, functools.partial(own_across, p)))
            for t in range(Z):
                events.append((base + t + ACROSS[t > 0], p, functools.partial(across, p, t)))
    events.sort(key=lambda e: e[0])
    last = [max(k for k, e in enumerate(events) if e[1] == p) for p in range(parts)]

    def wait_sibling(p, u):
        if C > 1:
            wait_recv(u * C + (C - 1) - c, p)

    def weigh(u):
        if u == 0:
            k_load.wait()
        wait_sibling(0, u)
        cols = pl.ds(u * C * rows, C * rows)
        block = o_all[u * C:(u + 1) * C].reshape(C * rows, o_all.shape[-1])
        density = lax.dot_general(
            o_all[me], block, (((1,), (1,)), ((), ())), preferred_element_type=jnp.float32
        )
        w[:, cols] = (density * k_v[:, cols].astype(jnp.float32)).astype(jnp.bfloat16)

    wide = 2 * LANES if groups % 2 == 0 else LANES
    depth = min(n, max(1, 2048 // rows))

    def apply(h, j):
        if j == 0:
            for u in range(units):
                wait_sibling(1 + h, u)
        cols = pl.ds(j * wide, wide)

        def term(q):
            block = b_all[h, pl.ds(q * depth, depth), :, cols].reshape(depth * rows, wide)
            return jnp.dot(
                w[:, pl.ds(pl.multiple_of(q * depth * rows, LANES), depth * rows)],
                block,
                preferred_element_type=jnp.float32,
            )

        if n == depth:
            total = term(0)
        else:
            total = lax.fori_loop(
                0, n // depth, lambda q, a: a + term(q), jnp.zeros((rows, wide), jnp.float32)
            )
        app_t[h, cols, :] = total.astype(jnp.bfloat16).T

    count = n // 2

    def exchange(h, q):
        qq = (q + me) % count
        s, e = qq // per, qq % per
        d = (2 * s + h) * per + e
        off = pl.multiple_of(s * LANES + e * cw, 16)
        return d, pltpu.make_async_remote_copy(
            src_ref=app_t.at[h, pl.ds(off, cw), :],
            dst_ref=got.at[:, pl.ds(pl.multiple_of(me * rows, LANES), rows)],
            send_sem=a2a_send.at[h, q],
            recv_sem=a2a_recv.at[me],
            device_id={"row": d},
            device_id_type=MESH,
        ), pltpu.make_async_copy(
            app_t.at[h, pl.ds(off, cw), :],
            got.at[:, pl.ds(pl.multiple_of(me * rows, LANES), rows)],
            a2a_recv.at[me],
        )

    def hand_out(h):
        for q in range(count):
            d, remote, local = exchange(h, q)
            pl.when(d != me)(lambda: remote.start())
            pl.when(d == me)(lambda: local.start())

    work = {p: [] for p in range(parts)}
    for u in range(units):
        work[0].append(functools.partial(weigh, u))
    for h in range(2):
        for j in range(half_cols // wide):
            work[1 + h].append(functools.partial(apply, h, j))
        work[1 + h].append(functools.partial(hand_out, h))

    queue = []
    for k, (_, _, event) in enumerate(events):
        event()
        if queue:
            queue.pop(0)()
        for p in range(parts):
            if last[p] == k:
                queue.extend(work[p])
    for item in queue:
        item()

    for src in range(n):
        pltpu.make_async_copy(
            got.at[:, pl.ds(src * rows, rows)], got.at[:, pl.ds(src * rows, rows)], a2a_recv.at[src]
        ).wait()
    for h in range(2):
        for j in range(half_cols // wide):
            cols = pl.ds(j * wide, wide)

            def term(q):
                block = b_all[h, pl.ds(q * depth, depth), :, cols].reshape(depth * rows, wide)
                return jnp.dot(
                    got[:, pl.ds(pl.multiple_of(q * depth * rows, LANES), depth * rows)],
                    block,
                    preferred_element_type=jnp.float32,
                )

            if n == depth:
                total = term(0)
            else:
                total = lax.fori_loop(
                    0, n // depth, lambda q, a: a + term(q), jnp.zeros((cw, wide), jnp.float32)
                )
            for v in range(wide // LANES):
                g = 2 * (j * (wide // LANES) + v) + h
                out_ref[:, pl.ds(g * LANES, LANES)] = total[:, v * LANES:(v + 1) * LANES]

    for h in range(2):
        for q in range(count):
            d, remote, _ = exchange(h, q)
            pl.when(d != me)(lambda: remote.wait_send())
    for p in range(parts):
        for zz in range(Z):
            i = index(zz, y, c)
            pl.when(jnp.logical_and(has_up, zz <= z))(lambda: copy(i, p, 0).wait_send())
            pl.when(jnp.logical_and(has_down, zz >= z))(lambda: copy(i, p, 1).wait_send())
            if Y > 1:
                pl.when(goes_across(zz, p))(lambda: copy(i, p, 2).wait_send())
        if relays:
            i = index(z, peer_y, c)
            pl.when(relay_up(p))(lambda: copy(i, p, 0).wait_send())
            pl.when(relay_down(p))(lambda: copy(i, p, 1).wait_send())
        if C > 1:
            for u in range(units):
                copy(u * C + c, p, 3).wait_send()


def routes(Z, Y, units):
    parents = {}
    for zs in range(Z):
        for ys in range(Y):
            for u in range(units):
                tree = {}
                for z in range(Z):
                    for y in range(Y):
                        if (z, y) == (zs, ys):
                            continue
                        if y == ys:
                            tree[z, y] = (z - 1, y) if z > zs else (z + 1, y)
                        elif (zs, z) in ((0, 1), (Z - 1, Z - 2)):
                            tree[z, y] = (zs, y)
                        elif (zs, z) in ((1, 0), (Z - 2, Z - 1)) and u % 2 == MOVED:
                            tree[z, y] = (zs, y)
                        else:
                            tree[z, y] = (z, ys)
                parents[zs, ys, u] = tree
    return parents


def timetable(Z, Y, units, step, hop):
    parents = routes(Z, Y, units)
    kids, height = {}, {}
    for key, tree in parents.items():
        children = {}
        for node, parent in tree.items():
            children.setdefault(parent, []).append(node)

        def depth(node):
            return max((1 + depth(child) for child in children.get(node, [])), default=0)

        kids[key] = children
        height[key] = {node: depth(node) for node in list(tree) + [key[:2]]}
    tick = 0
    queued, free, flying, starts, arrival = {}, {}, [], [], {}

    def have(node, key, now):
        arrival[node, key] = now
        for child in kids[key].get(node, []):
            inward = (key[0] - node[0]) * (1 if 2 * node[0] < Z else -1)
            rank = (key[2], -height[key][child], inward, key[1] == node[1])
            queued.setdefault((node, child), []).append((rank, key))

    for key in sorted(parents):
        have(key[:2], key, 0)
    while flying or any(queued.values()):
        landed = [f for f in flying if f[0] <= tick]
        flying = [f for f in flying if f[0] > tick]
        for _, node, key in landed:
            have(node, key, tick)
        for link, waiting in queued.items():
            if waiting and free.get(link, 0) <= tick:
                waiting.sort()
                _, key = waiting.pop(0)
                starts.append((tick, link, key))
                free[link] = tick + step
                flying.append((tick + step + hop, link[1], key))
        tick += 1
    return starts, arrival


def program(Z, Y, role, units, step, hop, ahead):
    starts, arrival = timetable(Z, Y, units, step, hop)
    node = (role, 0)
    passed = {key for _, link, key in starts if link[0] == node}
    moves = []
    for (where, key), when in arrival.items():
        if where == node and key[:2] != node:
            moves.append((when + (0 if key in passed else LAZY), 0, "take", key, None))
    latest = {}
    for when, (parent, child), key in starts:
        if parent == node:
            kind = 2 if child[1] != node[1] else (0 if child[0] > node[0] else 1)
            at = max(arrival[node, key], when - ahead, latest.get(kind, 0))
            latest[kind] = at
            moves.append((at, 1, "send", key, kind))
    moves.sort(key=lambda move: move[:2])
    return moves


def planned(
    dims, o_in, b_in, k_in, out_ref,
    o_all, b_all, k_v, w, app_t, got, in_sem, send_sem, recv_sem, a2a_send, a2a_recv,
):
    Z, Y, C = dims
    n = Z * Y * C
    rows = o_in.shape[0]
    blocks, wide = b_all.shape[0], b_all.shape[-1]
    cw = got.shape[1]
    owners = wide // cw
    cut = rows // OPARTS
    units = OPARTS + blocks
    order = sorted(range(blocks), key=lambda b: (min(b, blocks - 1 - b), b))
    roles = (Z + 1) // 2

    me = lax.axis_index("row")
    c = me % C
    y = (me // C) % Y
    z = me // (C * Y)
    low = 2 * z < Z
    role = jnp.minimum(z, Z - 1 - z)

    def index(zz, yy, cc):
        return (zz * Y + yy) * C + cc

    def place(zm):
        return jnp.where(low, zm, Z - 1 - zm)

    def device(key):
        return index(place(key[0]), y if key[1] == 0 else (Y - 1) - y, c)

    inner = index(place(jnp.minimum(role + 1, Z - 1)), y, c)
    outer = index(place(jnp.maximum(role - 1, 0)), y, c)
    y_dev = index(z, (Y - 1) - y, c)
    sib_dev = index(z, y, (C - 1) - c)

    def chunk(i, u):
        if u < OPARTS:
            return o_all.at[i, pl.ds(u * cut, cut)]
        return b_all.at[order[u - OPARTS], i]

    def copy(i, u, kind):
        return pltpu.make_async_remote_copy(
            src_ref=chunk(i, u),
            dst_ref=chunk(i, u),
            send_sem=send_sem.at[kind, u, i // C],
            recv_sem=recv_sem.at[u, i],
            device_id={"row": (inner, outer, y_dev, sib_dev)[kind]},
            device_id_type=MESH,
        )

    loads = []
    for u in range(units):
        if u < OPARTS:
            source = o_in.at[pl.ds(u * cut, cut)]
        else:
            source = b_in.at[:, pl.ds(order[u - OPARTS] * wide, wide)]
        loads.append(pltpu.make_async_copy(source, chunk(me, u), in_sem.at[u]))
    k_load = pltpu.make_async_copy(k_in, k_v, in_sem.at[units])
    for load in loads:
        load.start()
    k_load.start()

    barrier = pltpu.get_barrier_semaphore()

    def greet(dev):
        pl.semaphore_signal(barrier, inc=1, device_id={"row": dev}, device_id_type=MESH)

    greet(inner)
    pl.when(role > 0)(lambda: greet(outer))
    greet(y_dev)
    greet(sib_dev)
    pl.semaphore_wait(barrier, 3 + (role > 0).astype(jnp.int32))

    def weigh(chip):
        i = index(place(chip[0]), y if chip[1] == 0 else (Y - 1) - y, 0)
        span = pl.ds(pl.multiple_of(i * rows, LANES), C * rows)
        block = o_all[pl.ds(i, C)].reshape(C * rows, o_all.shape[-1])
        density = lax.dot_general(
            o_all[me], block, (((1,), (1,)), ((), ())), preferred_element_type=jnp.float32
        )
        w[:, span] = (density * k_v[:, span].astype(jnp.float32)).astype(jnp.bfloat16)

    def apply(b):
        total = jnp.dot(
            w[...], b_all[b].reshape(n * rows, wide), preferred_element_type=jnp.float32
        )
        app_t[b] = total.astype(jnp.bfloat16).T

    def exchange(b, q):
        e = (q + me) % owners
        d = b * owners + e
        source = app_t.at[b, pl.ds(pl.multiple_of(e * cw, 16), cw), :]
        target = got.at[me]
        return d, pltpu.make_async_remote_copy(
            src_ref=source,
            dst_ref=target,
            send_sem=a2a_send.at[b, q],
            recv_sem=a2a_recv.at[me],
            device_id={"row": d},
            device_id_type=MESH,
        ), lambda: pltpu.make_async_copy(source, target, a2a_recv.at[me])

    def hand_out(b):
        for q in range(owners):
            d, remote, local = exchange(b, q)
            pl.when(d != me)(remote.start)
            pl.when(d == me)(lambda: local().start())

    def from_sibling(key):
        i = device(key) - c + (C - 1) - c
        copy(i, key[2], 3).wait_recv()

    def run(moves, own):
        chips = [(zz, yy) for zz in range(Z) for yy in range(Y)]
        missing = {u: set(chips) for u in range(units)}
        seen, weighed, ready, loaded, whole, taken = set(), [], [], set(), {}, [0]

        def arrived(key):
            missing[key[2]].discard(key[:2])
            if key[2] < OPARTS and all(key[:2] not in missing[u] for u in range(OPARTS)):
                ready.append((taken[0], key))
            if not missing[key[2]]:
                whole[key[2]] = taken[0]

        def compute(age):
            for item in [r for r in ready if r[0] + age <= taken[0]]:
                ready.remove(item)
                chip = item[1][:2]
                if not weighed:
                    k_load.wait()
                for u in range(OPARTS):
                    from_sibling(chip + (u,))
                weigh(chip)
                weighed.append(chip)
            for s in range(blocks):
                u = OPARTS + s
                if len(weighed) == len(chips) and u in whole and whole[u] + age <= taken[0] and u not in seen:
                    seen.add(u)
                    for chip in chips:
                        from_sibling(chip + (u,))
                    apply(order[s])
                    hand_out(order[s])

        for u in range(units):
            arrived(own + (u,))

        for _, _, move, key, kind in moves:
            if move == "take":
                compute(AGE)
                copy(device(key), key[2], 3).wait_recv()
                copy(device(key), key[2], 3).start()
                taken[0] += 1
                arrived(key)
            else:
                if key[:2] == own and key[2] not in loaded:
                    loaded.add(key[2])
                    loads[key[2]].wait()
                    copy(me, key[2], 3).start()
                copy(device(key), key[2], kind).start()
        compute(0)

    plans = [program(Z, Y, r, units, STEP, HOP, AHEAD) for r in range(roles)]
    for r in range(roles):
        pl.when(role == r)(functools.partial(run, plans[r], (r, 0)))

    for src in range(n):
        pltpu.make_async_copy(
            got.at[src], got.at[src], a2a_recv.at[src]
        ).wait()
    mine = jnp.concatenate([got[src] for src in range(n)], axis=1)
    for b in range(blocks):
        out_ref[:, pl.ds(b * wide, wide)] = jnp.dot(
            mine, b_all[b].reshape(n * rows, wide), preferred_element_type=jnp.float32
        )

    for b in range(blocks):
        for q in range(owners):
            d, remote, _ = exchange(b, q)
            pl.when(d != me)(remote.wait_send)

    def drain(moves):
        for _, _, move, key, kind in moves:
            if move == "send":
                copy(device(key), key[2], kind).wait_send()

    for r in range(roles):
        pl.when(role == r)(functools.partial(drain, plans[r]))
    for u in range(units):
        for chip in range(Z * Y):
            copy(chip * C + c, u, 3).wait_send()


def planned_shards(dims, orbitals, basis, kernel_block):
    Z, Y, C = dims
    n = Z * Y * C
    rows, nocc = orbitals.shape
    nb = basis.shape[1]
    points = kernel_block.shape[1]
    wide = nb // Z
    cw = nb // n
    units = OPARTS + Z
    bf16 = jnp.bfloat16
    any_space = pl.BlockSpec(memory_space=pl.ANY)
    return pl.pallas_call(
        functools.partial(planned, dims),
        out_shape=jax.ShapeDtypeStruct((cw, nb), jnp.float32),
        in_specs=[any_space] * 3,
        out_specs=pl.BlockSpec(memory_space=pltpu.VMEM),
        scratch_shapes=[
            pltpu.VMEM((n, rows, nocc), bf16),
            pltpu.VMEM((Z, n, rows, wide), bf16),
            pltpu.VMEM((rows, points), bf16),
            pltpu.VMEM((rows, points), bf16),
            pltpu.VMEM((Z, wide, rows), bf16),
            pltpu.VMEM((n, cw, rows), bf16),
            pltpu.SemaphoreType.DMA((units + 1,)),
            pltpu.SemaphoreType.DMA((4, units, Z * Y)),
            pltpu.SemaphoreType.DMA((units, n)),
            pltpu.SemaphoreType.DMA((Z, wide // cw)),
            pltpu.SemaphoreType.DMA((n,)),
        ],
        compiler_params=pltpu.CompilerParams(
            collective_id=0, has_side_effects=True, vmem_limit_bytes=60 * 1024 * 1024
        ),
    )(orbitals, basis, kernel_block).T


def shards(dims, orbitals, basis, kernel_block):
    Z, Y, C = dims
    n = Z * Y * C
    rows, nocc = orbitals.shape
    nb = basis.shape[1]
    points = kernel_block.shape[1]
    whole = nb % (Z * LANES) == 0 and rows % (16 * OPARTS) == 0 and (nb // n) % 16 == 0
    if Y == 2 and C == 2 and Z // 2 == 2 and whole:
        return planned_shards(dims, orbitals, basis, kernel_block)
    half = nb // 2
    cw = nb // n
    bf16 = jnp.bfloat16
    any_space = pl.BlockSpec(memory_space=pl.ANY)
    return pl.pallas_call(
        functools.partial(kernel, dims),
        out_shape=jax.ShapeDtypeStruct((cw, nb), jnp.float32),
        in_specs=[any_space] * 3,
        out_specs=pl.BlockSpec(memory_space=pltpu.VMEM),
        scratch_shapes=[
            pltpu.VMEM((n, rows, nocc), bf16),
            pltpu.VMEM((2, n, rows, half), bf16),
            pltpu.VMEM((rows, points), bf16),
            pltpu.VMEM((rows, points), bf16),
            pltpu.VMEM((2, half, rows), bf16),
            pltpu.VMEM((cw, points), bf16),
            pltpu.SemaphoreType.DMA((2 + nb // LANES,)),
            pltpu.SemaphoreType.DMA((4, 3, Z * Y)),
            pltpu.SemaphoreType.DMA((3, n)),
            pltpu.SemaphoreType.DMA((2, n // 2)),
            pltpu.SemaphoreType.DMA((n,)),
        ],
        compiler_params=pltpu.CompilerParams(
            collective_id=0, has_side_effects=True, vmem_limit_bytes=60 * 1024 * 1024
        ),
    )(orbitals, basis, kernel_block).T


def solution(mesh):
    spec = P(("groups", "row"), None)
    return jax.shard_map(
        functools.partial(shards, layout(mesh)),
        mesh=mesh,
        in_specs=(spec, spec, spec),
        out_specs=P("groups", "row"),
        check_vma=False,
    )
```

```python
import functools

import jax
import jax.numpy as jnp
from jax import lax
from jax.experimental import pallas as pl
from jax.experimental.pallas import tpu as pltpu
from jax.sharding import PartitionSpec as P

LANES = 128
LEAD, LEAD_Y, LATE, ACROSS = (0, 7, 7), (0, 7, 7), 0, (2.1, 5.6)
MESH = pl.DeviceIdType.MESH
OPARTS, STEP, HOP, AHEAD, LAZY, MOVED, AGE = 2, 14, 32, 60, 60, 1, 4


def layout(mesh):
    n = mesh.shape["row"]
    try:
        line = mesh.devices[0]
        places = [tuple(d.coords) + (d.core_on_chip,) for d in line]
    except AttributeError:
        return n, 1, 1
    cores = len({p[-1] for p in places})
    axes = [a for a in range(3) if len({p[a] for p in places}) > 1]
    sizes = {a: len({p[a] for p in places}) for a in axes}
    for axis_z in axes:
        rest = [a for a in axes if a != axis_z]
        if len(rest) > 1 or (rest and sizes[rest[0]] != 2):
            continue
        y_size = sizes[rest[0]] if rest else 1
        z0 = min(p[axis_z] for p in places)
        y0 = min(p[rest[0]] for p in places) if rest else 0
        found = [
            ((p[axis_z] - z0) * y_size + (p[rest[0]] - y0 if rest else 0)) * cores + p[-1]
            for p in places
        ]
        if found == list(range(n)):
            return sizes[axis_z], y_size, cores
    return n, 1, 1


def kernel(
    dims, o_in, b_in, k_in, out_ref,
    o_all, b_all, k_v, w, app_t, got, in_sem, send_sem, recv_sem, a2a_send, a2a_recv,
):
    Z, Y, C = dims
    n = Z * Y * C
    units = Z * Y
    parts = 3
    rows = o_in.shape[0]
    half_cols = b_all.shape[-1]
    groups = half_cols // LANES
    cw = app_t.shape[0] * app_t.shape[1] // n
    per = LANES // cw

    me = lax.axis_index("row")
    c = me % C
    y = (me // C) % Y
    z = me // (C * Y)
    peer_y = (Y - 1) - y

    def index(zz, yy, cc):
        return (zz * Y + yy) * C + cc

    up_dev = index(jnp.minimum(z + 1, Z - 1), y, c)
    down_dev = index(jnp.maximum(z - 1, 0), y, c)
    y_dev = index(z, peer_y, c)
    sib_dev = index(z, y, (C - 1) - c)
    has_up = z < Z - 1
    has_down = z > 0

    def chunk(i, p):
        return o_all.at[i] if p == 0 else b_all.at[p - 1, i]

    def copy(i, p, kind):
        dev = (up_dev, down_dev, y_dev, sib_dev)[kind]
        return pltpu.make_async_remote_copy(
            src_ref=chunk(i, p),
            dst_ref=chunk(i, p),
            send_sem=send_sem.at[kind, p, i // C],
            recv_sem=recv_sem.at[p, i],
            device_id={"row": dev},
            device_id_type=MESH,
        )

    def wait_recv(i, p):
        copy(i, p, 3).wait_recv()

    loads = [pltpu.make_async_copy(o_in, o_all.at[me], in_sem.at[0])]
    for g in range(2 * groups):
        h, s = g % 2, g // 2
        loads.append(
            pltpu.make_async_copy(
                b_in.at[:, pl.ds(g * LANES, LANES)],
                b_all.at[h, me, :, pl.ds(s * LANES, LANES)],
                in_sem.at[1 + g],
            )
        )
    k_load = pltpu.make_async_copy(k_in, k_v, in_sem.at[1 + 2 * groups])
    for load in loads:
        load.start()
    k_load.start()

    barrier = pltpu.get_barrier_semaphore()

    def greet(dev):
        pl.semaphore_signal(barrier, inc=1, device_id={"row": dev}, device_id_type=MESH)

    pl.when(has_up)(lambda: greet(up_dev))
    pl.when(has_down)(lambda: greet(down_dev))
    if Y > 1:
        greet(y_dev)
    if C > 1:
        greet(sib_dev)
    others = (Y > 1) + (C > 1)
    pl.semaphore_wait(barrier, others + has_up.astype(jnp.int32) + has_down.astype(jnp.int32))

    relays = Y > 1 and Z >= 4
    both, either = jnp.logical_and, jnp.logical_or

    def goes_across(zz, p):
        if not relays:
            return True
        turn = c == p % C
        end = either(both(both(z == 0, zz == 1), turn), both(both(z == Z - 1, zz == Z - 2), turn))
        beside = either(both(z == 1, zz == 0), both(z == Z - 2, zz == Z - 1))
        return jnp.logical_not(either(end, beside))

    def relay_up(p):
        return either(z == 0, both(z == Z - 2, c == p % C))

    def relay_down(p):
        return either(z == Z - 1, both(z == 1, c == p % C))

    def spread(i, zz, p, up=False, down=False, across=False):
        if up:
            pl.when(has_up)(lambda: copy(i, p, 0).start())
        if down:
            pl.when(has_down)(lambda: copy(i, p, 1).start())
        if across and Y > 1:
            pl.when(goes_across(zz, p))(lambda: copy(i, p, 2).start())
        if C > 1:
            copy(i, p, 3).start()

    def own(p):
        if p == 0:
            loads[0].wait()
        else:
            for g in range(2 * groups):
                if g % 2 == p - 1:
                    loads[1 + g].wait()
        pl.when(has_up)(lambda: copy(me, p, 0).start())
        pl.when(has_down)(lambda: copy(me, p, 1).start())
        if C > 1:
            copy(me, p, 3).start()

    def own_across(p):
        copy(me, p, 2).start()

    def along(p, t):
        def low():
            i = index(z - t, y, c)
            wait_recv(i, p)
            spread(i, z - t, p, up=True, across=True)

        def high():
            i = index(z + t, y, c)
            wait_recv(i, p)
            spread(i, z + t, p, down=True, across=True)

        pl.when(z - t >= 0)(low)
        pl.when(z + t < Z)(high)

    def across(p, t):
        def one(zz):
            i = index(zz, peer_y, c)
            wait_recv(i, p)
            if relays and t == 0:
                pl.when(relay_up(p))(lambda: copy(i, p, 0).start())
                pl.when(relay_down(p))(lambda: copy(i, p, 1).start())
            spread(i, zz, p)

        if t == 0:
            one(z)
        else:
            pl.when(z - t >= 0)(lambda: one(z - t))
            pl.when(z + t < Z)(lambda: one(z + t))

    stride = (Z - 0.5) if relays else (Z if Y > 1 else max(Z - 1, 1))
    events = []
    for p in range(parts):
        base = p * stride
        events.append((base - LEAD[p], p, functools.partial(own, p)))
        for t in range(1, Z):
            events.append((base + t + LATE * (t > 1), p, functools.partial(along, p, t)))
        if Y > 1:
            events.append((base - LEAD_Y[p] + 0.01, p, functools.partial(own_across, p)))
            for t in range(Z):
                events.append((base + t + ACROSS[t > 0], p, functools.partial(across, p, t)))
    events.sort(key=lambda e: e[0])
    last = [max(k for k, e in enumerate(events) if e[1] == p) for p in range(parts)]

    def wait_sibling(p, u):
        if C > 1:
            wait_recv(u * C + (C - 1) - c, p)

    def weigh(u):
        if u == 0:
            k_load.wait()
        wait_sibling(0, u)
        cols = pl.ds(u * C * rows, C * rows)
        block = o_all[u * C:(u + 1) * C].reshape(C * rows, o_all.shape[-1])
        density = lax.dot_general(
            o_all[me], block, (((1,), (1,)), ((), ())), preferred_element_type=jnp.float32
        )
        w[:, cols] = (density * k_v[:, cols].astype(jnp.float32)).astype(jnp.bfloat16)

    wide = 2 * LANES if groups % 2 == 0 else LANES
    depth = min(n, max(1, 2048 // rows))

    def apply(h, j):
        if j == 0:
            for u in range(units):
                wait_sibling(1 + h, u)
        cols = pl.ds(j * wide, wide)

        def term(q):
            block = b_all[h, pl.ds(q * depth, depth), :, cols].reshape(depth * rows, wide)
            return jnp.dot(
                w[:, pl.ds(pl.multiple_of(q * depth * rows, LANES), depth * rows)],
                block,
                preferred_element_type=jnp.float32,
            )

        if n == depth:
            total = term(0)
        else:
            total = lax.fori_loop(
                0, n // depth, lambda q, a: a + term(q), jnp.zeros((rows, wide), jnp.float32)
            )
        app_t[h, cols, :] = total.astype(jnp.bfloat16).T

    count = n // 2

    def exchange(h, q):
        qq = (q + me) % count
        s, e = qq // per, qq % per
        d = (2 * s + h) * per + e
        off = pl.multiple_of(s * LANES + e * cw, 16)
        return d, pltpu.make_async_remote_copy(
            src_ref=app_t.at[h, pl.ds(off, cw), :],
            dst_ref=got.at[:, pl.ds(pl.multiple_of(me * rows, LANES), rows)],
            send_sem=a2a_send.at[h, q],
            recv_sem=a2a_recv.at[me],
            device_id={"row": d},
            device_id_type=MESH,
        ), pltpu.make_async_copy(
            app_t.at[h, pl.ds(off, cw), :],
            got.at[:, pl.ds(pl.multiple_of(me * rows, LANES), rows)],
            a2a_recv.at[me],
        )

    def hand_out(h):
        for q in range(count):
            d, remote, local = exchange(h, q)
            pl.when(d != me)(lambda: remote.start())
            pl.when(d == me)(lambda: local.start())

    work = {p: [] for p in range(parts)}
    for u in range(units):
        work[0].append(functools.partial(weigh, u))
    for h in range(2):
        for j in range(half_cols // wide):
            work[1 + h].append(functools.partial(apply, h, j))
        work[1 + h].append(functools.partial(hand_out, h))

    queue = []
    for k, (_, _, event) in enumerate(events):
        event()
        if queue:
            queue.pop(0)()
        for p in range(parts):
            if last[p] == k:
                queue.extend(work[p])
    for item in queue:
        item()

    for src in range(n):
        pltpu.make_async_copy(
            got.at[:, pl.ds(src * rows, rows)], got.at[:, pl.ds(src * rows, rows)], a2a_recv.at[src]
        ).wait()
    for h in range(2):
        for j in range(half_cols // wide):
            cols = pl.ds(j * wide, wide)

            def term(q):
                block = b_all[h, pl.ds(q * depth, depth), :, cols].reshape(depth * rows, wide)
                return jnp.dot(
                    got[:, pl.ds(pl.multiple_of(q * depth * rows, LANES), depth * rows)],
                    block,
                    preferred_element_type=jnp.float32,
                )

            if n == depth:
                total = term(0)
            else:
                total = lax.fori_loop(
                    0, n // depth, lambda q, a: a + term(q), jnp.zeros((cw, wide), jnp.float32)
                )
            for v in range(wide // LANES):
                g = 2 * (j * (wide // LANES) + v) + h
                out_ref[:, pl.ds(g * LANES, LANES)] = total[:, v * LANES:(v + 1) * LANES]

    for h in range(2):
        for q in range(count):
            d, remote, _ = exchange(h, q)
            pl.when(d != me)(lambda: remote.wait_send())
    for p in range(parts):
        for zz in range(Z):
            i = index(zz, y, c)
            pl.when(jnp.logical_and(has_up, zz <= z))(lambda: copy(i, p, 0).wait_send())
            pl.when(jnp.logical_and(has_down, zz >= z))(lambda: copy(i, p, 1).wait_send())
            if Y > 1:
                pl.when(goes_across(zz, p))(lambda: copy(i, p, 2).wait_send())
        if relays:
            i = index(z, peer_y, c)
            pl.when(relay_up(p))(lambda: copy(i, p, 0).wait_send())
            pl.when(relay_down(p))(lambda: copy(i, p, 1).wait_send())
        if C > 1:
            for u in range(units):
                copy(u * C + c, p, 3).wait_send()


def routes(Z, Y, units):
    parents = {}
    for zs in range(Z):
        for ys in range(Y):
            for u in range(units):
                tree = {}
                for z in range(Z):
                    for y in range(Y):
                        if (z, y) == (zs, ys):
                            continue
                        if y == ys:
                            tree[z, y] = (z - 1, y) if z > zs else (z + 1, y)
                        elif (zs, z) in ((0, 1), (Z - 1, Z - 2)):
                            tree[z, y] = (zs, y)
                        elif (zs, z) in ((1, 0), (Z - 2, Z - 1)) and u % 2 == MOVED:
                            tree[z, y] = (zs, y)
                        else:
                            tree[z, y] = (z, ys)
                parents[zs, ys, u] = tree
    return parents


def timetable(Z, Y, units, step, hop):
    parents = routes(Z, Y, units)
    kids, height = {}, {}
    for key, tree in parents.items():
        children = {}
        for node, parent in tree.items():
            children.setdefault(parent, []).append(node)

        def depth(node):
            return max((1 + depth(child) for child in children.get(node, [])), default=0)

        kids[key] = children
        height[key] = {node: depth(node) for node in list(tree) + [key[:2]]}
    tick = 0
    queued, free, flying, starts, arrival = {}, {}, [], [], {}

    def have(node, key, now):
        arrival[node, key] = now
        for child in kids[key].get(node, []):
            inward = (key[0] - node[0]) * (1 if 2 * node[0] < Z else -1)
            rank = (2 * key[2] - height[key][child], key[2], inward, key[1] == node[1])
            queued.setdefault((node, child), []).append((rank, key))

    for key in sorted(parents):
        have(key[:2], key, 0)
    while flying or any(queued.values()):
        landed = [f for f in flying if f[0] <= tick]
        flying = [f for f in flying if f[0] > tick]
        for _, node, key in landed:
            have(node, key, tick)
        for link, waiting in queued.items():
            if waiting and free.get(link, 0) <= tick:
                waiting.sort()
                _, key = waiting.pop(0)
                starts.append((tick, link, key))
                free[link] = tick + step
                flying.append((tick + step + hop, link[1], key))
        tick += 1
    return starts, arrival


def program(Z, Y, role, units, step, hop, ahead):
    starts, arrival = timetable(Z, Y, units, step, hop)
    node = (role, 0)
    passed = {key for _, link, key in starts if link[0] == node}
    moves = []
    for (where, key), when in arrival.items():
        if where == node and key[:2] != node:
            moves.append((when + (0 if key in passed else LAZY), 0, "take", key, None))
    latest = {}
    for when, (parent, child), key in starts:
        if parent == node:
            kind = 2 if child[1] != node[1] else (0 if child[0] > node[0] else 1)
            at = max(arrival[node, key], when - ahead, latest.get(kind, 0))
            latest[kind] = at
            moves.append((at, 1, "send", key, kind))
    moves.sort(key=lambda move: move[:2])
    return moves


def planned(
    dims, o_in, b_in, k_in, out_ref,
    o_all, b_all, k_v, w, app_t, got, in_sem, send_sem, recv_sem, a2a_send, a2a_recv,
):
    Z, Y, C = dims
    n = Z * Y * C
    rows = o_in.shape[0]
    blocks, wide = b_all.shape[0], b_all.shape[-1]
    cw = got.shape[1]
    owners = wide // cw
    cut = rows // OPARTS
    units = OPARTS + blocks
    order = sorted(range(blocks), key=lambda b: (min(b, blocks - 1 - b), b))
    roles = (Z + 1) // 2

    me = lax.axis_index("row")
    c = me % C
    y = (me // C) % Y
    z = me // (C * Y)
    low = 2 * z < Z
    role = jnp.minimum(z, Z - 1 - z)

    def index(zz, yy, cc):
        return (zz * Y + yy) * C + cc

    def place(zm):
        return jnp.where(low, zm, Z - 1 - zm)

    def device(key):
        return index(place(key[0]), y if key[1] == 0 else (Y - 1) - y, c)

    inner = index(place(jnp.minimum(role + 1, Z - 1)), y, c)
    outer = index(place(jnp.maximum(role - 1, 0)), y, c)
    y_dev = index(z, (Y - 1) - y, c)
    sib_dev = index(z, y, (C - 1) - c)

    def chunk(i, u):
        if u < OPARTS:
            return o_all.at[i, pl.ds(u * cut, cut)]
        return b_all.at[order[u - OPARTS], i]

    def copy(i, u, kind):
        return pltpu.make_async_remote_copy(
            src_ref=chunk(i, u),
            dst_ref=chunk(i, u),
            send_sem=send_sem.at[kind, u, i // C],
            recv_sem=recv_sem.at[u, i],
            device_id={"row": (inner, outer, y_dev, sib_dev)[kind]},
            device_id_type=MESH,
        )

    loads = []
    for u in range(units):
        if u < OPARTS:
            source = o_in.at[pl.ds(u * cut, cut)]
        else:
            source = b_in.at[:, pl.ds(order[u - OPARTS] * wide, wide)]
        loads.append(pltpu.make_async_copy(source, chunk(me, u), in_sem.at[u]))
    k_load = pltpu.make_async_copy(k_in, k_v, in_sem.at[units])
    for load in loads:
        load.start()
    k_load.start()

    barrier = pltpu.get_barrier_semaphore()

    def greet(dev):
        pl.semaphore_signal(barrier, inc=1, device_id={"row": dev}, device_id_type=MESH)

    greet(inner)
    pl.when(role > 0)(lambda: greet(outer))
    greet(y_dev)
    greet(sib_dev)
    pl.semaphore_wait(barrier, 3 + (role > 0).astype(jnp.int32))

    def weigh(chip):
        i = index(place(chip[0]), y if chip[1] == 0 else (Y - 1) - y, 0)
        span = pl.ds(pl.multiple_of(i * rows, LANES), C * rows)
        block = o_all[pl.ds(i, C)].reshape(C * rows, o_all.shape[-1])
        density = lax.dot_general(
            o_all[me], block, (((1,), (1,)), ((), ())), preferred_element_type=jnp.float32
        )
        w[:, span] = (density * k_v[:, span].astype(jnp.float32)).astype(jnp.bfloat16)

    def apply(b):
        total = jnp.dot(
            w[...], b_all[b].reshape(n * rows, wide), preferred_element_type=jnp.float32
        )
        app_t[b] = total.astype(jnp.bfloat16).T

    def exchange(b, q):
        e = (q + me) % owners
        d = b * owners + e
        source = app_t.at[b, pl.ds(pl.multiple_of(e * cw, 16), cw), :]
        target = got.at[me]
        return d, pltpu.make_async_remote_copy(
            src_ref=source,
            dst_ref=target,
            send_sem=a2a_send.at[b, q],
            recv_sem=a2a_recv.at[me],
            device_id={"row": d},
            device_id_type=MESH,
        ), lambda: pltpu.make_async_copy(source, target, a2a_recv.at[me])

    def hand_out(b):
        for q in range(owners):
            d, remote, local = exchange(b, q)
            pl.when(d != me)(remote.start)
            pl.when(d == me)(lambda: local().start())

    def from_sibling(key):
        i = device(key) - c + (C - 1) - c
        copy(i, key[2], 3).wait_recv()

    def run(moves, own):
        chips = [(zz, yy) for zz in range(Z) for yy in range(Y)]
        missing = {u: set(chips) for u in range(units)}
        seen, weighed, ready, loaded, whole, taken = set(), [], [], set(), {}, [0]

        def arrived(key):
            missing[key[2]].discard(key[:2])
            if key[2] < OPARTS and all(key[:2] not in missing[u] for u in range(OPARTS)):
                ready.append((taken[0], key))
            if not missing[key[2]]:
                whole[key[2]] = taken[0]

        def compute(age):
            for item in [r for r in ready if r[0] + age <= taken[0]]:
                ready.remove(item)
                chip = item[1][:2]
                if not weighed:
                    k_load.wait()
                for u in range(OPARTS):
                    from_sibling(chip + (u,))
                weigh(chip)
                weighed.append(chip)
            for s in range(blocks):
                u = OPARTS + s
                if len(weighed) == len(chips) and u in whole and whole[u] + age <= taken[0] and u not in seen:
                    seen.add(u)
                    for chip in chips:
                        from_sibling(chip + (u,))
                    apply(order[s])
                    hand_out(order[s])

        for u in range(units):
            arrived(own + (u,))

        for _, _, move, key, kind in moves:
            if move == "take":
                compute(AGE)
                copy(device(key), key[2], 3).wait_recv()
                copy(device(key), key[2], 3).start()
                taken[0] += 1
                arrived(key)
            else:
                if key[:2] == own and key[2] not in loaded:
                    loaded.add(key[2])
                    loads[key[2]].wait()
                    copy(me, key[2], 3).start()
                copy(device(key), key[2], kind).start()
        compute(0)

    plans = [program(Z, Y, r, units, STEP, HOP, AHEAD) for r in range(roles)]
    for r in range(roles):
        pl.when(role == r)(functools.partial(run, plans[r], (r, 0)))

    for src in range(n):
        pltpu.make_async_copy(
            got.at[src], got.at[src], a2a_recv.at[src]
        ).wait()
    mine = jnp.concatenate([got[src] for src in range(n)], axis=1)
    for b in range(blocks):
        out_ref[:, pl.ds(b * wide, wide)] = jnp.dot(
            mine, b_all[b].reshape(n * rows, wide), preferred_element_type=jnp.float32
        )

    for b in range(blocks):
        for q in range(owners):
            d, remote, _ = exchange(b, q)
            pl.when(d != me)(remote.wait_send)

    def drain(moves):
        for _, _, move, key, kind in moves:
            if move == "send":
                copy(device(key), key[2], kind).wait_send()

    for r in range(roles):
        pl.when(role == r)(functools.partial(drain, plans[r]))
    for u in range(units):
        for chip in range(Z * Y):
            copy(chip * C + c, u, 3).wait_send()


def planned_shards(dims, orbitals, basis, kernel_block):
    Z, Y, C = dims
    n = Z * Y * C
    rows, nocc = orbitals.shape
    nb = basis.shape[1]
    points = kernel_block.shape[1]
    wide = nb // Z
    cw = nb // n
    units = OPARTS + Z
    bf16 = jnp.bfloat16
    any_space = pl.BlockSpec(memory_space=pl.ANY)
    return pl.pallas_call(
        functools.partial(planned, dims),
        out_shape=jax.ShapeDtypeStruct((cw, nb), jnp.float32),
        in_specs=[any_space] * 3,
        out_specs=pl.BlockSpec(memory_space=pltpu.VMEM),
        scratch_shapes=[
            pltpu.VMEM((n, rows, nocc), bf16),
            pltpu.VMEM((Z, n, rows, wide), bf16),
            pltpu.VMEM((rows, points), bf16),
            pltpu.VMEM((rows, points), bf16),
            pltpu.VMEM((Z, wide, rows), bf16),
            pltpu.VMEM((n, cw, rows), bf16),
            pltpu.SemaphoreType.DMA((units + 1,)),
            pltpu.SemaphoreType.DMA((4, units, Z * Y)),
            pltpu.SemaphoreType.DMA((units, n)),
            pltpu.SemaphoreType.DMA((Z, wide // cw)),
            pltpu.SemaphoreType.DMA((n,)),
        ],
        compiler_params=pltpu.CompilerParams(
            collective_id=0, has_side_effects=True, vmem_limit_bytes=60 * 1024 * 1024
        ),
    )(orbitals, basis, kernel_block).T


def shards(dims, orbitals, basis, kernel_block):
    Z, Y, C = dims
    n = Z * Y * C
    rows, nocc = orbitals.shape
    nb = basis.shape[1]
    points = kernel_block.shape[1]
    whole = nb % (Z * LANES) == 0 and rows % (16 * OPARTS) == 0 and (nb // n) % 16 == 0
    if Y == 2 and C == 2 and Z // 2 == 2 and whole:
        return planned_shards(dims, orbitals, basis, kernel_block)
    half = nb // 2
    cw = nb // n
    bf16 = jnp.bfloat16
    any_space = pl.BlockSpec(memory_space=pl.ANY)
    return pl.pallas_call(
        functools.partial(kernel, dims),
        out_shape=jax.ShapeDtypeStruct((cw, nb), jnp.float32),
        in_specs=[any_space] * 3,
        out_specs=pl.BlockSpec(memory_space=pltpu.VMEM),
        scratch_shapes=[
            pltpu.VMEM((n, rows, nocc), bf16),
            pltpu.VMEM((2, n, rows, half), bf16),
            pltpu.VMEM((rows, points), bf16),
            pltpu.VMEM((rows, points), bf16),
            pltpu.VMEM((2, half, rows), bf16),
            pltpu.VMEM((cw, points), bf16),
            pltpu.SemaphoreType.DMA((2 + nb // LANES,)),
            pltpu.SemaphoreType.DMA((4, 3, Z * Y)),
            pltpu.SemaphoreType.DMA((3, n)),
            pltpu.SemaphoreType.DMA((2, n // 2)),
            pltpu.SemaphoreType.DMA((n,)),
        ],
        compiler_params=pltpu.CompilerParams(
            collective_id=0, has_side_effects=True, vmem_limit_bytes=60 * 1024 * 1024
        ),
    )(orbitals, basis, kernel_block).T


def solution(mesh):
    spec = P(("groups", "row"), None)
    return jax.shard_map(
        functools.partial(shards, layout(mesh)),
        mesh=mesh,
        in_specs=(spec, spec, spec),
        out_specs=P("groups", "row"),
        check_vma=False,
    )
```

```python
import functools

import jax
import jax.numpy as jnp
from jax import lax
from jax.experimental import pallas as pl
from jax.experimental.pallas import tpu as pltpu
from jax.sharding import PartitionSpec as P

LANES = 128
LEAD, LEAD_Y, LATE, ACROSS = (0, 7, 7), (0, 7, 7), 0, (2.1, 5.6)
MESH = pl.DeviceIdType.MESH
OPARTS, STEP, HOP, AHEAD, LAZY, MOVED, AGE = 2, 14, 32, 60, 60, 1, 4


def layout(mesh):
    n = mesh.shape["row"]
    try:
        line = mesh.devices[0]
        places = [tuple(d.coords) + (d.core_on_chip,) for d in line]
    except AttributeError:
        return n, 1, 1
    cores = len({p[-1] for p in places})
    axes = [a for a in range(3) if len({p[a] for p in places}) > 1]
    sizes = {a: len({p[a] for p in places}) for a in axes}
    for axis_z in axes:
        rest = [a for a in axes if a != axis_z]
        if len(rest) > 1 or (rest and sizes[rest[0]] != 2):
            continue
        y_size = sizes[rest[0]] if rest else 1
        z0 = min(p[axis_z] for p in places)
        y0 = min(p[rest[0]] for p in places) if rest else 0
        found = [
            ((p[axis_z] - z0) * y_size + (p[rest[0]] - y0 if rest else 0)) * cores + p[-1]
            for p in places
        ]
        if found == list(range(n)):
            return sizes[axis_z], y_size, cores
    return n, 1, 1


def kernel(
    dims, o_in, b_in, k_in, out_ref,
    o_all, b_all, k_v, w, app_t, got, in_sem, send_sem, recv_sem, a2a_send, a2a_recv,
):
    Z, Y, C = dims
    n = Z * Y * C
    units = Z * Y
    parts = 3
    rows = o_in.shape[0]
    half_cols = b_all.shape[-1]
    groups = half_cols // LANES
    cw = app_t.shape[0] * app_t.shape[1] // n
    per = LANES // cw

    me = lax.axis_index("row")
    c = me % C
    y = (me // C) % Y
    z = me // (C * Y)
    peer_y = (Y - 1) - y

    def index(zz, yy, cc):
        return (zz * Y + yy) * C + cc

    up_dev = index(jnp.minimum(z + 1, Z - 1), y, c)
    down_dev = index(jnp.maximum(z - 1, 0), y, c)
    y_dev = index(z, peer_y, c)
    sib_dev = index(z, y, (C - 1) - c)
    has_up = z < Z - 1
    has_down = z > 0

    def chunk(i, p):
        return o_all.at[i] if p == 0 else b_all.at[p - 1, i]

    def copy(i, p, kind):
        dev = (up_dev, down_dev, y_dev, sib_dev)[kind]
        return pltpu.make_async_remote_copy(
            src_ref=chunk(i, p),
            dst_ref=chunk(i, p),
            send_sem=send_sem.at[kind, p, i // C],
            recv_sem=recv_sem.at[p, i],
            device_id={"row": dev},
            device_id_type=MESH,
        )

    def wait_recv(i, p):
        copy(i, p, 3).wait_recv()

    loads = [pltpu.make_async_copy(o_in, o_all.at[me], in_sem.at[0])]
    for g in range(2 * groups):
        h, s = g % 2, g // 2
        loads.append(
            pltpu.make_async_copy(
                b_in.at[:, pl.ds(g * LANES, LANES)],
                b_all.at[h, me, :, pl.ds(s * LANES, LANES)],
                in_sem.at[1 + g],
            )
        )
    k_load = pltpu.make_async_copy(k_in, k_v, in_sem.at[1 + 2 * groups])
    for load in loads:
        load.start()
    k_load.start()

    barrier = pltpu.get_barrier_semaphore()

    def greet(dev):
        pl.semaphore_signal(barrier, inc=1, device_id={"row": dev}, device_id_type=MESH)

    pl.when(has_up)(lambda: greet(up_dev))
    pl.when(has_down)(lambda: greet(down_dev))
    if Y > 1:
        greet(y_dev)
    if C > 1:
        greet(sib_dev)
    others = (Y > 1) + (C > 1)
    pl.semaphore_wait(barrier, others + has_up.astype(jnp.int32) + has_down.astype(jnp.int32))

    relays = Y > 1 and Z >= 4
    both, either = jnp.logical_and, jnp.logical_or

    def goes_across(zz, p):
        if not relays:
            return True
        turn = c == p % C
        end = either(both(both(z == 0, zz == 1), turn), both(both(z == Z - 1, zz == Z - 2), turn))
        beside = either(both(z == 1, zz == 0), both(z == Z - 2, zz == Z - 1))
        return jnp.logical_not(either(end, beside))

    def relay_up(p):
        return either(z == 0, both(z == Z - 2, c == p % C))

    def relay_down(p):
        return either(z == Z - 1, both(z == 1, c == p % C))

    def spread(i, zz, p, up=False, down=False, across=False):
        if up:
            pl.when(has_up)(lambda: copy(i, p, 0).start())
        if down:
            pl.when(has_down)(lambda: copy(i, p, 1).start())
        if across and Y > 1:
            pl.when(goes_across(zz, p))(lambda: copy(i, p, 2).start())
        if C > 1:
            copy(i, p, 3).start()

    def own(p):
        if p == 0:
            loads[0].wait()
        else:
            for g in range(2 * groups):
                if g % 2 == p - 1:
                    loads[1 + g].wait()
        pl.when(has_up)(lambda: copy(me, p, 0).start())
        pl.when(has_down)(lambda: copy(me, p, 1).start())
        if C > 1:
            copy(me, p, 3).start()

    def own_across(p):
        copy(me, p, 2).start()

    def along(p, t):
        def low():
            i = index(z - t, y, c)
            wait_recv(i, p)
            spread(i, z - t, p, up=True, across=True)

        def high():
            i = index(z + t, y, c)
            wait_recv(i, p)
            spread(i, z + t, p, down=True, across=True)

        pl.when(z - t >= 0)(low)
        pl.when(z + t < Z)(high)

    def across(p, t):
        def one(zz):
            i = index(zz, peer_y, c)
            wait_recv(i, p)
            if relays and t == 0:
                pl.when(relay_up(p))(lambda: copy(i, p, 0).start())
                pl.when(relay_down(p))(lambda: copy(i, p, 1).start())
            spread(i, zz, p)

        if t == 0:
            one(z)
        else:
            pl.when(z - t >= 0)(lambda: one(z - t))
            pl.when(z + t < Z)(lambda: one(z + t))

    stride = (Z - 0.5) if relays else (Z if Y > 1 else max(Z - 1, 1))
    events = []
    for p in range(parts):
        base = p * stride
        events.append((base - LEAD[p], p, functools.partial(own, p)))
        for t in range(1, Z):
            events.append((base + t + LATE * (t > 1), p, functools.partial(along, p, t)))
        if Y > 1:
            events.append((base - LEAD_Y[p] + 0.01, p, functools.partial(own_across, p)))
            for t in range(Z):
                events.append((base + t + ACROSS[t > 0], p, functools.partial(across, p, t)))
    events.sort(key=lambda e: e[0])
    last = [max(k for k, e in enumerate(events) if e[1] == p) for p in range(parts)]

    def wait_sibling(p, u):
        if C > 1:
            wait_recv(u * C + (C - 1) - c, p)

    def weigh(u):
        if u == 0:
            k_load.wait()
        wait_sibling(0, u)
        cols = pl.ds(u * C * rows, C * rows)
        block = o_all[u * C:(u + 1) * C].reshape(C * rows, o_all.shape[-1])
        density = lax.dot_general(
            o_all[me], block, (((1,), (1,)), ((), ())), preferred_element_type=jnp.float32
        )
        w[:, cols] = (density * k_v[:, cols].astype(jnp.float32)).astype(jnp.bfloat16)

    wide = 2 * LANES if groups % 2 == 0 else LANES
    depth = min(n, max(1, 2048 // rows))

    def apply(h, j):
        if j == 0:
            for u in range(units):
                wait_sibling(1 + h, u)
        cols = pl.ds(j * wide, wide)

        def term(q):
            block = b_all[h, pl.ds(q * depth, depth), :, cols].reshape(depth * rows, wide)
            return jnp.dot(
                w[:, pl.ds(pl.multiple_of(q * depth * rows, LANES), depth * rows)],
                block,
                preferred_element_type=jnp.float32,
            )

        if n == depth:
            total = term(0)
        else:
            total = lax.fori_loop(
                0, n // depth, lambda q, a: a + term(q), jnp.zeros((rows, wide), jnp.float32)
            )
        app_t[h, cols, :] = total.astype(jnp.bfloat16).T

    count = n // 2

    def exchange(h, q):
        qq = (q + me) % count
        s, e = qq // per, qq % per
        d = (2 * s + h) * per + e
        off = pl.multiple_of(s * LANES + e * cw, 16)
        return d, pltpu.make_async_remote_copy(
            src_ref=app_t.at[h, pl.ds(off, cw), :],
            dst_ref=got.at[:, pl.ds(pl.multiple_of(me * rows, LANES), rows)],
            send_sem=a2a_send.at[h, q],
            recv_sem=a2a_recv.at[me],
            device_id={"row": d},
            device_id_type=MESH,
        ), pltpu.make_async_copy(
            app_t.at[h, pl.ds(off, cw), :],
            got.at[:, pl.ds(pl.multiple_of(me * rows, LANES), rows)],
            a2a_recv.at[me],
        )

    def hand_out(h):
        for q in range(count):
            d, remote, local = exchange(h, q)
            pl.when(d != me)(lambda: remote.start())
            pl.when(d == me)(lambda: local.start())

    work = {p: [] for p in range(parts)}
    for u in range(units):
        work[0].append(functools.partial(weigh, u))
    for h in range(2):
        for j in range(half_cols // wide):
            work[1 + h].append(functools.partial(apply, h, j))
        work[1 + h].append(functools.partial(hand_out, h))

    queue = []
    for k, (_, _, event) in enumerate(events):
        event()
        if queue:
            queue.pop(0)()
        for p in range(parts):
            if last[p] == k:
                queue.extend(work[p])
    for item in queue:
        item()

    for src in range(n):
        pltpu.make_async_copy(
            got.at[:, pl.ds(src * rows, rows)], got.at[:, pl.ds(src * rows, rows)], a2a_recv.at[src]
        ).wait()
    for h in range(2):
        for j in range(half_cols // wide):
            cols = pl.ds(j * wide, wide)

            def term(q):
                block = b_all[h, pl.ds(q * depth, depth), :, cols].reshape(depth * rows, wide)
                return jnp.dot(
                    got[:, pl.ds(pl.multiple_of(q * depth * rows, LANES), depth * rows)],
                    block,
                    preferred_element_type=jnp.float32,
                )

            if n == depth:
                total = term(0)
            else:
                total = lax.fori_loop(
                    0, n // depth, lambda q, a: a + term(q), jnp.zeros((cw, wide), jnp.float32)
                )
            for v in range(wide // LANES):
                g = 2 * (j * (wide // LANES) + v) + h
                out_ref[:, pl.ds(g * LANES, LANES)] = total[:, v * LANES:(v + 1) * LANES]

    for h in range(2):
        for q in range(count):
            d, remote, _ = exchange(h, q)
            pl.when(d != me)(lambda: remote.wait_send())
    for p in range(parts):
        for zz in range(Z):
            i = index(zz, y, c)
            pl.when(jnp.logical_and(has_up, zz <= z))(lambda: copy(i, p, 0).wait_send())
            pl.when(jnp.logical_and(has_down, zz >= z))(lambda: copy(i, p, 1).wait_send())
            if Y > 1:
                pl.when(goes_across(zz, p))(lambda: copy(i, p, 2).wait_send())
        if relays:
            i = index(z, peer_y, c)
            pl.when(relay_up(p))(lambda: copy(i, p, 0).wait_send())
            pl.when(relay_down(p))(lambda: copy(i, p, 1).wait_send())
        if C > 1:
            for u in range(units):
                copy(u * C + c, p, 3).wait_send()


def routes(Z, Y, units):
    parents = {}
    for zs in range(Z):
        for ys in range(Y):
            for u in range(units):
                tree = {}
                for z in range(Z):
                    for y in range(Y):
                        if (z, y) == (zs, ys):
                            continue
                        if y == ys:
                            tree[z, y] = (z - 1, y) if z > zs else (z + 1, y)
                        elif (zs, z) in ((0, 1), (Z - 1, Z - 2)):
                            tree[z, y] = (zs, y)
                        elif (zs, z) in ((1, 0), (Z - 2, Z - 1)) and u % 2 == MOVED:
                            tree[z, y] = (zs, y)
                        else:
                            tree[z, y] = (z, ys)
                parents[zs, ys, u] = tree
    return parents


def timetable(Z, Y, units, step, hop):
    parents = routes(Z, Y, units)
    kids, height = {}, {}
    for key, tree in parents.items():
        children = {}
        for node, parent in tree.items():
            children.setdefault(parent, []).append(node)

        def depth(node):
            return max((1 + depth(child) for child in children.get(node, [])), default=0)

        kids[key] = children
        height[key] = {node: depth(node) for node in list(tree) + [key[:2]]}
    tick = 0
    queued, free, flying, starts, arrival = {}, {}, [], [], {}

    def have(node, key, now):
        arrival[node, key] = now
        for child in kids[key].get(node, []):
            inward = (key[0] - node[0]) * (1 if 2 * node[0] < Z else -1)
            rank = (key[2], key[:2] == node, -height[key][child], inward, key[1] == node[1])
            queued.setdefault((node, child), []).append((rank, key))

    for key in sorted(parents):
        have(key[:2], key, 0)
    while flying or any(queued.values()):
        landed = [f for f in flying if f[0] <= tick]
        flying = [f for f in flying if f[0] > tick]
        for _, node, key in landed:
            have(node, key, tick)
        for link, waiting in queued.items():
            if waiting and free.get(link, 0) <= tick:
                waiting.sort()
                _, key = waiting.pop(0)
                starts.append((tick, link, key))
                free[link] = tick + step
                flying.append((tick + step + hop, link[1], key))
        tick += 1
    return starts, arrival


def program(Z, Y, role, units, step, hop, ahead):
    starts, arrival = timetable(Z, Y, units, step, hop)
    node = (role, 0)
    passed = {key for _, link, key in starts if link[0] == node}
    moves = []
    for (where, key), when in arrival.items():
        if where == node and key[:2] != node:
            moves.append((when + (0 if key in passed else LAZY), 0, "take", key, None))
    latest = {}
    for when, (parent, child), key in starts:
        if parent == node:
            kind = 2 if child[1] != node[1] else (0 if child[0] > node[0] else 1)
            at = max(arrival[node, key], when - ahead, latest.get(kind, 0))
            latest[kind] = at
            moves.append((at, 1, "send", key, kind))
    moves.sort(key=lambda move: move[:2])
    return moves


def planned(
    dims, o_in, b_in, k_in, out_ref,
    o_all, b_all, k_v, w, app_t, got, in_sem, send_sem, recv_sem, a2a_send, a2a_recv,
):
    Z, Y, C = dims
    n = Z * Y * C
    rows = o_in.shape[0]
    blocks, wide = b_all.shape[0], b_all.shape[-1]
    cw = got.shape[1]
    owners = wide // cw
    cut = rows // OPARTS
    units = OPARTS + blocks
    order = sorted(range(blocks), key=lambda b: (min(b, blocks - 1 - b), b))
    roles = (Z + 1) // 2

    me = lax.axis_index("row")
    c = me % C
    y = (me // C) % Y
    z = me // (C * Y)
    low = 2 * z < Z
    role = jnp.minimum(z, Z - 1 - z)

    def index(zz, yy, cc):
        return (zz * Y + yy) * C + cc

    def place(zm):
        return jnp.where(low, zm, Z - 1 - zm)

    def device(key):
        return index(place(key[0]), y if key[1] == 0 else (Y - 1) - y, c)

    inner = index(place(jnp.minimum(role + 1, Z - 1)), y, c)
    outer = index(place(jnp.maximum(role - 1, 0)), y, c)
    y_dev = index(z, (Y - 1) - y, c)
    sib_dev = index(z, y, (C - 1) - c)

    def chunk(i, u):
        if u < OPARTS:
            return o_all.at[i, pl.ds(u * cut, cut)]
        return b_all.at[order[u - OPARTS], i]

    def copy(i, u, kind):
        return pltpu.make_async_remote_copy(
            src_ref=chunk(i, u),
            dst_ref=chunk(i, u),
            send_sem=send_sem.at[kind, u, i // C],
            recv_sem=recv_sem.at[u, i],
            device_id={"row": (inner, outer, y_dev, sib_dev)[kind]},
            device_id_type=MESH,
        )

    loads = []
    for u in range(units):
        if u < OPARTS:
            source = o_in.at[pl.ds(u * cut, cut)]
        else:
            source = b_in.at[:, pl.ds(order[u - OPARTS] * wide, wide)]
        loads.append(pltpu.make_async_copy(source, chunk(me, u), in_sem.at[u]))
    k_load = pltpu.make_async_copy(k_in, k_v, in_sem.at[units])
    for load in loads:
        load.start()
    k_load.start()

    barrier = pltpu.get_barrier_semaphore()

    def greet(dev):
        pl.semaphore_signal(barrier, inc=1, device_id={"row": dev}, device_id_type=MESH)

    greet(inner)
    pl.when(role > 0)(lambda: greet(outer))
    greet(y_dev)
    greet(sib_dev)
    pl.semaphore_wait(barrier, 3 + (role > 0).astype(jnp.int32))

    def weigh(chip):
        i = index(place(chip[0]), y if chip[1] == 0 else (Y - 1) - y, 0)
        span = pl.ds(pl.multiple_of(i * rows, LANES), C * rows)
        block = o_all[pl.ds(i, C)].reshape(C * rows, o_all.shape[-1])
        density = lax.dot_general(
            o_all[me], block, (((1,), (1,)), ((), ())), preferred_element_type=jnp.float32
        )
        w[:, span] = (density * k_v[:, span].astype(jnp.float32)).astype(jnp.bfloat16)

    def apply(b):
        total = jnp.dot(
            w[...], b_all[b].reshape(n * rows, wide), preferred_element_type=jnp.float32
        )
        app_t[b] = total.astype(jnp.bfloat16).T

    def exchange(b, q):
        e = (q + me) % owners
        d = b * owners + e
        source = app_t.at[b, pl.ds(pl.multiple_of(e * cw, 16), cw), :]
        target = got.at[me]
        return d, pltpu.make_async_remote_copy(
            src_ref=source,
            dst_ref=target,
            send_sem=a2a_send.at[b, q],
            recv_sem=a2a_recv.at[me],
            device_id={"row": d},
            device_id_type=MESH,
        ), lambda: pltpu.make_async_copy(source, target, a2a_recv.at[me])

    def hand_out(b):
        for q in range(owners):
            d, remote, local = exchange(b, q)
            pl.when(d != me)(remote.start)
            pl.when(d == me)(lambda: local().start())

    def from_sibling(key):
        i = device(key) - c + (C - 1) - c
        copy(i, key[2], 3).wait_recv()

    def run(moves, own):
        chips = [(zz, yy) for zz in range(Z) for yy in range(Y)]
        missing = {u: set(chips) for u in range(units)}
        seen, weighed, ready, loaded, whole, taken = set(), [], [], set(), {}, [0]

        def arrived(key):
            missing[key[2]].discard(key[:2])
            if key[2] < OPARTS and all(key[:2] not in missing[u] for u in range(OPARTS)):
                ready.append((taken[0], key))
            if not missing[key[2]]:
                whole[key[2]] = taken[0]

        def compute(age):
            for item in [r for r in ready if r[0] + age <= taken[0]]:
                ready.remove(item)
                chip = item[1][:2]
                if not weighed:
                    k_load.wait()
                for u in range(OPARTS):
                    from_sibling(chip + (u,))
                weigh(chip)
                weighed.append(chip)
            for s in range(blocks):
                u = OPARTS + s
                if len(weighed) == len(chips) and u in whole and whole[u] + age <= taken[0] and u not in seen:
                    seen.add(u)
                    for chip in chips:
                        from_sibling(chip + (u,))
                    apply(order[s])
                    hand_out(order[s])

        for u in range(units):
            arrived(own + (u,))

        for _, _, move, key, kind in moves:
            if move == "take":
                compute(AGE)
                copy(device(key), key[2], 3).wait_recv()
                copy(device(key), key[2], 3).start()
                taken[0] += 1
                arrived(key)
            else:
                if key[:2] == own and key[2] not in loaded:
                    loaded.add(key[2])
                    loads[key[2]].wait()
                    copy(me, key[2], 3).start()
                copy(device(key), key[2], kind).start()
        compute(0)

    plans = [program(Z, Y, r, units, STEP, HOP, AHEAD) for r in range(roles)]
    for r in range(roles):
        pl.when(role == r)(functools.partial(run, plans[r], (r, 0)))

    for src in range(n):
        pltpu.make_async_copy(
            got.at[src], got.at[src], a2a_recv.at[src]
        ).wait()
    mine = jnp.concatenate([got[src] for src in range(n)], axis=1)
    for b in range(blocks):
        out_ref[:, pl.ds(b * wide, wide)] = jnp.dot(
            mine, b_all[b].reshape(n * rows, wide), preferred_element_type=jnp.float32
        )

    for b in range(blocks):
        for q in range(owners):
            d, remote, _ = exchange(b, q)
            pl.when(d != me)(remote.wait_send)

    def drain(moves):
        for _, _, move, key, kind in moves:
            if move == "send":
                copy(device(key), key[2], kind).wait_send()

    for r in range(roles):
        pl.when(role == r)(functools.partial(drain, plans[r]))
    for u in range(units):
        for chip in range(Z * Y):
            copy(chip * C + c, u, 3).wait_send()


def planned_shards(dims, orbitals, basis, kernel_block):
    Z, Y, C = dims
    n = Z * Y * C
    rows, nocc = orbitals.shape
    nb = basis.shape[1]
    points = kernel_block.shape[1]
    wide = nb // Z
    cw = nb // n
    units = OPARTS + Z
    bf16 = jnp.bfloat16
    any_space = pl.BlockSpec(memory_space=pl.ANY)
    return pl.pallas_call(
        functools.partial(planned, dims),
        out_shape=jax.ShapeDtypeStruct((cw, nb), jnp.float32),
        in_specs=[any_space] * 3,
        out_specs=pl.BlockSpec(memory_space=pltpu.VMEM),
        scratch_shapes=[
            pltpu.VMEM((n, rows, nocc), bf16),
            pltpu.VMEM((Z, n, rows, wide), bf16),
            pltpu.VMEM((rows, points), bf16),
            pltpu.VMEM((rows, points), bf16),
            pltpu.VMEM((Z, wide, rows), bf16),
            pltpu.VMEM((n, cw, rows), bf16),
            pltpu.SemaphoreType.DMA((units + 1,)),
            pltpu.SemaphoreType.DMA((4, units, Z * Y)),
            pltpu.SemaphoreType.DMA((units, n)),
            pltpu.SemaphoreType.DMA((Z, wide // cw)),
            pltpu.SemaphoreType.DMA((n,)),
        ],
        compiler_params=pltpu.CompilerParams(
            collective_id=0, has_side_effects=True, vmem_limit_bytes=60 * 1024 * 1024
        ),
    )(orbitals, basis, kernel_block).T


def shards(dims, orbitals, basis, kernel_block):
    Z, Y, C = dims
    n = Z * Y * C
    rows, nocc = orbitals.shape
    nb = basis.shape[1]
    points = kernel_block.shape[1]
    whole = nb % (Z * LANES) == 0 and rows % (16 * OPARTS) == 0 and (nb // n) % 16 == 0
    if Y == 2 and C == 2 and Z // 2 == 2 and whole:
        return planned_shards(dims, orbitals, basis, kernel_block)
    half = nb // 2
    cw = nb // n
    bf16 = jnp.bfloat16
    any_space = pl.BlockSpec(memory_space=pl.ANY)
    return pl.pallas_call(
        functools.partial(kernel, dims),
        out_shape=jax.ShapeDtypeStruct((cw, nb), jnp.float32),
        in_specs=[any_space] * 3,
        out_specs=pl.BlockSpec(memory_space=pltpu.VMEM),
        scratch_shapes=[
            pltpu.VMEM((n, rows, nocc), bf16),
            pltpu.VMEM((2, n, rows, half), bf16),
            pltpu.VMEM((rows, points), bf16),
            pltpu.VMEM((rows, points), bf16),
            pltpu.VMEM((2, half, rows), bf16),
            pltpu.VMEM((cw, points), bf16),
            pltpu.SemaphoreType.DMA((2 + nb // LANES,)),
            pltpu.SemaphoreType.DMA((4, 3, Z * Y)),
            pltpu.SemaphoreType.DMA((3, n)),
            pltpu.SemaphoreType.DMA((2, n // 2)),
            pltpu.SemaphoreType.DMA((n,)),
        ],
        compiler_params=pltpu.CompilerParams(
            collective_id=0, has_side_effects=True, vmem_limit_bytes=60 * 1024 * 1024
        ),
    )(orbitals, basis, kernel_block).T


def solution(mesh):
    spec = P(("groups", "row"), None)
    return jax.shard_map(
        functools.partial(shards, layout(mesh)),
        mesh=mesh,
        in_specs=(spec, spec, spec),
        out_specs=P("groups", "row"),
        check_vma=False,
    )
```
